256 devices in a mesh: outer: 8 (over y, core), inner: 32 (over x, z).
Axes of the slice: x: 4, y: 4, z: 8, core: 2. Of those that a mesh axis runs over, the one named last changes fastest.
Arguments:
- queries: bfloat16 [131072, 16, 128], P(('outer', 'inner')), may hold values from -1.5 to 1.5
- key_vectors: bfloat16 [131072, 16, 128], P(('outer', 'inner')), may hold values from -1.5 to 1.5
- value_vectors: bfloat16 [131072, 16, 128], P(('outer', 'inner')), may hold values from -6 to 6
- level_weights: float32 [18, 16, 131072], P(None, None, ('outer', 'inner')), may hold values from 0.25 to 1
Outputs:
- attended: bfloat16 [131072, 16, 128], P(('outer', 'inner'))
The draws below stay inside these ranges and needn't reach their ends.
All inputs are finite; a program needn't handle non-finite values.
Results may differ from the reference program's by a relative error of at most 0.0049.
Values may be sent and summed in bfloat16 or wider, within the bound.
A program may use at most 128 MiB of HBM per device.

```python
import math
import jax
import jax.numpy as jnp
from jax import lax

HEADS = 16
HDIM = 128
LEVELS = 18
TOK_BITS = 9
TOK_DEV = 512
TOKENS = 131072


def level_of(own_key, shape, split, low, top_value):
    loudness = 1.0
    for dim, shards_of in split:
        steps = jax.random.uniform(jax.random.fold_in(jax.random.fold_in(own_key, 6), dim), (shards_of,), jnp.float32, low / len(split), top_value / len(split))
        loudness = loudness * jnp.repeat(jnp.exp(steps), shape[dim] // shards_of).reshape((-1,) + (1,) * (len(shape) - 1 - dim))
    return loudness


def normal_values(stream_key, dims, deviation, most, shards=(), kind=jnp.bfloat16):
    factor_of = level_of(stream_key, dims, shards, -0.22, 0.18) if shards else 1.0
    values = jax.random.normal(stream_key, dims, jnp.float32) * deviation * factor_of
    return jnp.minimum(jnp.maximum(values, -most), most).astype(kind)


def setup_inputs(seed: int = 0) -> dict:
    keys = jax.random.split(jax.random.key(seed), 5)
    queries = normal_values(keys[0], (TOKENS, HEADS, HDIM), 0.25, 1.5, ((0, 256),))
    key_vectors = normal_values(keys[1], (TOKENS, HEADS, HDIM), 0.25, 1.5, ((0, 256),))
    value_vectors = normal_values(keys[2], (TOKENS, HEADS, HDIM), 1.0, 6.0, ((0, 256),))
    level_weights = jnp.clip(jnp.exp(math.log(1.0) - 1.3862944 * jax.random.uniform(keys[3], (LEVELS, HEADS, TOKENS), jnp.float32) ** level_of(keys[3], (LEVELS, HEADS, TOKENS), ((2, 256),), -0.2, 0.2)), 0.25, 1.0)
    return dict(queries=queries, key_vectors=key_vectors, value_vectors=value_vectors, level_weights=level_weights)


def level_table(block_len):
    position = jnp.arange(block_len, dtype=jnp.int32)
    differ = position[:, None] ^ position[None, :]
    levels_at = jnp.zeros((block_len, block_len), jnp.int32)
    for bit_pos in range(block_len.bit_length() - 1):
        levels_at = levels_at + (differ >= (1 << bit_pos)).astype(jnp.int32)
    causal = position[None, :] <= position[:, None]
    return levels_at, causal


def scaled_gains(level_weights):
    count = level_weights.shape[0]
    factor = jnp.exp2(-0.5 * jnp.arange(count, dtype=jnp.float32))
    return level_weights * factor[:, None, None]


def local_terms(queries, key_vectors, value_vectors, gains):
    block_len = queries.shape[0]
    levels_at, causal = level_table(block_len)
    scores = jnp.einsum("thd,shd->hts", queries.astype(jnp.float32), key_vectors.astype(jnp.float32))
    weighting = jnp.zeros(scores.shape, jnp.float32)
    for level_idx in range(block_len.bit_length()):
        weighting = weighting + jnp.where((levels_at == level_idx)[None], gains[level_idx][:, :, None], jnp.float32(0.0))
    attn_weights = jnp.where(causal[None], scores * weighting, jnp.float32(0.0)).astype(jnp.bfloat16)
    return jnp.einsum("hts,shd->thd", attn_weights.astype(jnp.float32), value_vectors.astype(jnp.float32))


def reference(queries, key_vectors, value_vectors, level_weights):
    blocks = TOKENS // TOK_DEV
    depth = (blocks - 1).bit_length()
    gains = scaled_gains(level_weights)
    q_blocks = queries.reshape(blocks, TOK_DEV, HEADS, HDIM)
    k_blocks = key_vectors.reshape(blocks, TOK_DEV, HEADS, HDIM)
    v_blocks = value_vectors.reshape(blocks, TOK_DEV, HEADS, HDIM)
    gain_blocks = gains.reshape(LEVELS, HEADS, blocks, TOK_DEV).transpose(2, 0, 1, 3)

    def block_state(pair):
        return jnp.einsum("shd,she->hde", pair[0].astype(jnp.float32), pair[1].astype(jnp.float32))

    tiers = [lax.map(block_state, (k_blocks, v_blocks))]
    for step_idx in range(depth - 1):
        lower = tiers[-1]
        tiers.append(lower[0::2] + lower[1::2])

    def one_block(inputs):
        place, q_blk, k_blk, v_blk, gain_blk = inputs
        output_sum = local_terms(q_blk, k_blk, v_blk, gain_blk)
        for bit_pos in range(depth):
            switch = ((place >> bit_pos) & 1).astype(jnp.float32)
            sibling = ((place >> bit_pos) ^ 1).astype(jnp.int32)
            bucket = lax.dynamic_index_in_dim(tiers[bit_pos], sibling, 0, keepdims=False).astype(jnp.bfloat16)
            contrib = jnp.einsum("thd,hde->the", q_blk.astype(jnp.float32), bucket.astype(jnp.float32))
            level_gain = gain_blk[TOK_BITS + 1 + bit_pos] * switch
            output_sum = output_sum + contrib * level_gain.T[:, :, None]
        return output_sum.astype(jnp.bfloat16)

    places = jnp.arange(blocks, dtype=jnp.int32)
    result = lax.map(one_block, (places, q_blocks, k_blocks, v_blocks, gain_blocks))
    return result.reshape(TOKENS, HEADS, HDIM)
```

```python
import math

import jax
import jax.numpy as jnp
from jax import lax
from jax.experimental import pallas as pl
from jax.experimental.pallas import tpu as pltpu
from jax.sharding import PartitionSpec as P

MESH = pl.DeviceIdType.MESH
F32 = jnp.float32
BF16 = jnp.bfloat16

T = 512
H = 16
D = 128
TIERS = 8
LEVELS = 18
LOCAL_BITS = 9
TILE = 128
HOP = 2
DELAY = [HOP * tier for tier in range(TIERS + 1)]
TICKS = H + DELAY[TIERS]
FACTOR = [2.0 ** (-0.5 * level) for level in range(LEVELS)]


def dot_nt(a, b):
    return lax.dot_general(a, b, (((1,), (1,)), ((), ())), preferred_element_type=F32)


def dot_nn(a, b):
    return lax.dot_general(a, b, (((1,), (0,)), ((), ())), preferred_element_type=F32)


def either(value, *options):
    found = value == options[0]
    for option in options[1:]:
        found = jnp.logical_or(found, value == option)
    return found


def kernel(
    q_hbm, k_hbm, v_hbm, lw_hbm, o_hbm,
    x_in, k_in, v_in, lw, q32, k32, v32, qh, kh, vt, wt, acc, outs,
    run, sent, got, in_sem, out_sem, send_sem, extra_sem, recv_sem,
):
    outer = lax.axis_index("outer")
    inner = lax.axis_index("inner")
    core = lax.rem(outer, 2)
    y = lax.div(outer, 2)
    z = lax.rem(inner, 8)
    x = lax.div(inner, 8)
    p = lax.rem(z, 4)
    place = outer * 32 + inner

    copies = [
        pltpu.make_async_copy(k_hbm, k_in, in_sem.at[0]),
        pltpu.make_async_copy(v_hbm, v_in, in_sem.at[1]),
        pltpu.make_async_copy(lw_hbm, lw, in_sem.at[2]),
        pltpu.make_async_copy(q_hbm, x_in, in_sem.at[3]),
    ]
    for copy in copies:
        copy.start()

    def flip(value):
        return value + 1 - 2 * lax.rem(value, 2)

    def at(zz, xx, yy, cc):
        return (yy * 2 + cc, xx * 8 + zz)

    base4 = z - p
    source1 = base4 + jnp.where(p < 2, 2, 1)
    second1 = base4 + jnp.where(p == 1, 3, 0)
    serves1 = either(p, 1, 2)
    source2 = jnp.where(either(z, 0, 1), 7, jnp.where(either(z, 6, 7), 0, jnp.where(either(z, 2, 3), 4, 3)))
    second2 = jnp.where(z == 0, 6, jnp.where(z == 7, 1, jnp.where(z == 3, 5, 2)))
    serves2 = either(z, 0, 3, 4, 7)

    partner = [
        at(flip(z), x, y, core),
        at(source1, x, y, core),
        at(source2, x, y, core),
        at(z, flip(x), y, core),
        at(z, 3 - x, y, core),
        at(z, x, y, 1 - core),
        at(z, x, flip(y), core),
        at(z, x, 3 - y, core),
    ]
    second = {1: at(second1, x, y, core), 2: at(second2, x, y, core)}
    serves = {1: serves1, 2: serves2}

    barrier = pltpu.get_barrier_semaphore()
    for tier in range(TIERS):
        pl.semaphore_signal(barrier, inc=1, device_id=partner[tier], device_id_type=MESH)
    for tier in (1, 2):
        @pl.when(serves[tier])
        def _(tier=tier):
            pl.semaphore_signal(barrier, inc=1, device_id=second[tier], device_id_type=MESH)

    def send(tier, c, device, sem):
        return pltpu.make_async_remote_copy(
            src_ref=sent.at[tier, c],
            dst_ref=got.at[tier, c],
            send_sem=sem,
            recv_sem=recv_sem.at[tier, c],
            device_id=device,
            device_id_type=MESH,
        )

    def start_sends(tier, c):
        if tier in serves:
            @pl.when(serves[tier])
            def _():
                send(tier, c, partner[tier], send_sem.at[tier]).start()
                send(tier, c, second[tier], extra_sem.at[tier]).start()
        else:
            send(tier, c, partner[tier], send_sem.at[tier]).start()

    def widen(source, target):
        def step(i, carry):
            rows = source[pl.ds(i * 32, 32)].astype(F32).reshape(32 * H, D)
            target[pl.ds(pl.multiple_of(i * 32 * H, 32 * H), 32 * H), :] = rows
            return carry
        lax.fori_loop(0, T // 32, step, 0)

    def head_of(source, c):
        return source[pl.ds(c, T, stride=H), :].astype(BF16)

    copies[0].wait()
    widen(k_in, k32)
    copies[1].wait()
    widen(v_in, v32)
    wt[pl.ds(TILE, TILE), pl.ds(0, TILE)] = jnp.zeros((TILE, TILE), BF16)
    wt[pl.ds(3 * TILE, TILE), pl.ds(2 * TILE, TILE)] = jnp.zeros((TILE, TILE), BF16)

    waits = 8 + serves1.astype(jnp.int32) + serves2.astype(jnp.int32)
    pl.semaphore_wait(barrier, waits)

    lane = lax.rem(lax.broadcasted_iota(jnp.int32, (16, T), 1), TILE)
    group = lax.broadcasted_iota(jnp.int32, (16, T), 0)
    coarse = lax.shift_right_logical(lane, 3)
    coarse_diff = jnp.bitwise_xor(coarse, group)
    low_lane = lax.rem(lax.broadcasted_iota(jnp.int32, (8, T), 1), 8)
    low_row = lax.broadcasted_iota(jnp.int32, (8, T), 0)
    low_diff = jnp.bitwise_xor(low_lane, low_row)

    def gain(level, c):
        return lw[level, pl.ds(c, 1), :] * FACTOR[level]

    def local(c):
        q = head_of(q32, c)
        qh[c] = q
        keys = kh[c]
        wide = jnp.zeros((16, T), F32)
        for level in (4, 5, 6, 7):
            wide = jnp.where(coarse_diff >= (1 << (level - 4)), gain(level, c), wide)
        wide = jnp.where(coarse > group, wide, 0.0)
        narrow = jnp.broadcast_to(gain(0, c), (8, T))
        for level in (1, 2, 3):
            narrow = jnp.where(low_diff >= (1 << (level - 1)), gain(level, c), narrow)
        narrow = jnp.where(low_lane >= low_row, narrow, 0.0)
        gain8 = gain(8, c)
        gain9 = gain(9, c)
        shape3 = (16, 8, TILE)
        same = lax.shift_right_logical(lax.broadcasted_iota(jnp.int32, shape3, 2), 3) == lax.broadcasted_iota(
            jnp.int32, shape3, 0
        )
        for j in range(T // TILE):
            scores = dot_nt(keys[j * TILE:(j + 1) * TILE], q[j * TILE:])
            for i in range(j, T // TILE):
                cols = slice(i * TILE, (i + 1) * TILE)
                part = scores[:, (i - j) * TILE:(i - j + 1) * TILE]
                if i == j:
                    weight = jnp.where(
                        same,
                        jnp.broadcast_to(narrow[:, cols].reshape(1, 8, TILE), shape3),
                        jnp.broadcast_to(wide[:, cols].reshape(16, 1, TILE), shape3),
                    ).reshape(TILE, TILE)
                    part = part * weight
                elif i ^ j == 1:
                    part = part * gain8[:, cols]
                else:
                    part = part * gain9[:, cols]
                wt[pl.ds(j * TILE, TILE), pl.ds(i * TILE, TILE)] = part.astype(BF16)
        values = vt[c]
        half = T // 2
        acc[c, :, pl.ds(0, half)] = dot_nn(values[:, :half], wt[pl.ds(0, half), pl.ds(0, half)])
        acc[c, :, pl.ds(half, half)] = dot_nn(values, wt[:, pl.ds(half, half)])

    switches = [
        jnp.bitwise_and(lax.shift_right_logical(place, tier), 1).astype(F32) for tier in range(TIERS)
    ]

    def finish(c):
        half = T // 2
        for part in range(2):
            cols = pl.ds(part * half, half)
            q = qh[c, pl.ds(part * half, half), :]
            total = acc[c, :, cols]
            for tier in range(TIERS):
                row = lw[LOCAL_BITS + 1 + tier, pl.ds(c, 1), cols] * (
                    switches[tier] * FACTOR[LOCAL_BITS + 1 + tier]
                )
                total = total + dot_nt(got[tier, c], q) * row
            outs[c, pl.ds(part * half, half), :] = total.T.astype(BF16)
        pltpu.make_async_copy(outs.at[c], o_hbm.at[c], out_sem.at[c]).start()

    def active(t, tier):
        return jnp.logical_and(t >= DELAY[tier], t < DELAY[tier] + H)

    def tick(t, carry):
        @pl.when(active(t, 0))
        def _():
            keys = head_of(k32, t)
            kh[t] = keys
            values = v32[pl.ds(t, T, stride=H), :].T.astype(BF16)
            vt[t] = values
            state = dot_nn(values, keys)
            run[t] = state
            sent[0, t] = state.astype(BF16)

        for tier in range(1, TIERS):
            @pl.when(active(t, tier))
            def _(tier=tier):
                c = t - DELAY[tier]
                send(tier - 1, c, partner[tier - 1], send_sem.at[tier - 1]).wait_recv()
                total = run[c] + got[tier - 1, c].astype(F32)
                run[c] = total
                sent[tier, c] = total.astype(BF16)

        for tier in range(TIERS):
            @pl.when(active(t, tier))
            def _(tier=tier):
                start_sends(tier, t - DELAY[tier])

        @pl.when(active(t, 0))
        def _():
            @pl.when(t == 0)
            def _():
                copies[2].wait()
                copies[3].wait()
                widen(x_in, q32)
            local(t)

        @pl.when(active(t, TIERS))
        def _():
            c = t - DELAY[TIERS]
            send(TIERS - 1, c, partner[TIERS - 1], send_sem.at[TIERS - 1]).wait_recv()
            finish(c)

        return carry

    lax.fori_loop(0, TICKS, tick, 0)

    def whole(tier, device, sem):
        return pltpu.make_async_remote_copy(
            src_ref=sent.at[tier],
            dst_ref=got.at[tier],
            send_sem=sem,
            recv_sem=recv_sem.at[tier, 0],
            device_id=device,
            device_id_type=MESH,
        )

    for tier in range(TIERS):
        if tier in serves:
            @pl.when(serves[tier])
            def _(tier=tier):
                whole(tier, partner[tier], send_sem.at[tier]).wait_send()
                whole(tier, second[tier], extra_sem.at[tier]).wait_send()
        else:
            whole(tier, partner[tier], send_sem.at[tier]).wait_send()

    def drain(c, carry):
        pltpu.make_async_copy(outs.at[c], o_hbm.at[c], out_sem.at[c]).wait()
        return carry

    lax.fori_loop(0, H, drain, 0)


def per_device(queries, key_vectors, value_vectors, level_weights):
    hbm = pl.BlockSpec(memory_space=pl.ANY)
    by_head = pl.pallas_call(
        kernel,
        out_shape=jax.ShapeDtypeStruct((H, T, D), BF16),
        in_specs=[hbm] * 4,
        out_specs=hbm,
        scratch_shapes=[
            pltpu.VMEM((T, H, D), BF16),
            pltpu.VMEM((T, H, D), BF16),
            pltpu.VMEM((T, H, D), BF16),
            pltpu.VMEM((LEVELS, H, T), F32),
            pltpu.VMEM((T * H, D), F32),
            pltpu.VMEM((T * H, D), F32),
            pltpu.VMEM((T * H, D), F32),
            pltpu.VMEM((H, T, D), BF16),
            pltpu.VMEM((H, T, D), BF16),
            pltpu.VMEM((H, D, T), BF16),
            pltpu.VMEM((T, T), BF16),
            pltpu.VMEM((H, D, T), F32),
            pltpu.VMEM((H, T, D), BF16),
            pltpu.VMEM((H, D, D), F32),
            pltpu.VMEM((TIERS, H, D, D), BF16),
            pltpu.VMEM((TIERS, H, D, D), BF16),
            pltpu.SemaphoreType.DMA((4,)),
            pltpu.SemaphoreType.DMA((H,)),
            pltpu.SemaphoreType.DMA((TIERS,)),
            pltpu.SemaphoreType.DMA((TIERS,)),
            pltpu.SemaphoreType.DMA((TIERS, H)),
        ],
        compiler_params=pltpu.CompilerParams(
            collective_id=0, has_side_effects=True, vmem_limit_bytes=60 * 1024 * 1024
        ),
    )(queries, key_vectors, value_vectors, level_weights)
    return jnp.transpose(by_head, (1, 0, 2))


def solution(mesh):
    placed = (
        P(("outer", "inner"), None, None),
        P(("outer", "inner"), None, None),
        P(("outer", "inner"), None, None),
        P(None, None, ("outer", "inner")),
    )
    return jax.shard_map(
        per_device,
        mesh=mesh,
        in_specs=placed,
        out_specs=P(("outer", "inner"), None, None),
        check_vma=False,
    )
```

```python
import math

import jax
import jax.numpy as jnp
from jax import lax
from jax.experimental import pallas as pl
from jax.experimental.pallas import tpu as pltpu
from jax.sharding import PartitionSpec as P

MESH = pl.DeviceIdType.MESH
F32 = jnp.float32
BF16 = jnp.bfloat16

T = 512
H = 16
D = 128
TIERS = 8
LEVELS = 18
LOCAL_BITS = 9
TILE = 128
STAGES = 6
SLOTS = 10
DELAY = [0, 3, 6, 9, 12, 14, 17]
LOCAL_AT = 0
TICKS = H + DELAY[STAGES]
FACTOR = [2.0 ** (-0.5 * level) for level in range(LEVELS)]


def dot_nt(a, b):
    return lax.dot_general(a, b, (((1,), (1,)), ((), ())), preferred_element_type=F32)


def dot_nn(a, b):
    return lax.dot_general(a, b, (((1,), (0,)), ((), ())), preferred_element_type=F32)


def either(value, *options):
    found = value == options[0]
    for option in options[1:]:
        found = jnp.logical_or(found, value == option)
    return found


def kernel(
    q_hbm, k_hbm, v_hbm, lw_hbm, out,
    x_in, k_in, v_in, lw, q32, k32, v32, qh, kh, vt, wt, acc,
    run, sent, got, in_sem, send_sem, recv_sem,
):
    outer = lax.axis_index("outer")
    inner = lax.axis_index("inner")
    core = lax.rem(outer, 2)
    y = lax.div(outer, 2)
    z = lax.rem(inner, 8)
    x = lax.div(inner, 8)
    p = lax.rem(z, 4)
    place = outer * 32 + inner

    copies = [
        pltpu.make_async_copy(k_hbm, k_in, in_sem.at[0]),
        pltpu.make_async_copy(v_hbm, v_in, in_sem.at[1]),
        pltpu.make_async_copy(lw_hbm, lw, in_sem.at[2]),
        pltpu.make_async_copy(q_hbm, x_in, in_sem.at[3]),
    ]
    for copy in copies:
        copy.start()

    def flip(value):
        return value + 1 - 2 * lax.rem(value, 2)

    def at(zz, xx, yy, cc):
        return (yy * 2 + cc, xx * 8 + zz)

    base4 = z - p
    source1 = base4 + jnp.where(p < 2, 2, 1)
    second1 = base4 + jnp.where(p == 1, 3, 0)
    serves1 = either(p, 1, 2)
    source2 = jnp.where(either(z, 0, 1), 7, jnp.where(either(z, 6, 7), 0, jnp.where(either(z, 2, 3), 4, 3)))
    second2 = jnp.where(z == 0, 6, jnp.where(z == 7, 1, jnp.where(z == 3, 5, 2)))
    serves2 = either(z, 0, 3, 4, 7)

    far_y = lax.rem(y + 2, 4)
    far_x = lax.rem(x + 2, 4)
    routes = [
        [(0, at(flip(z), x, y, core), None)],
        [(1, at(second1, x, y, core), serves1), (1, at(source1, x, y, core), serves1)],
        [(2, at(second2, x, y, core), serves2), (2, at(source2, x, y, core), serves2)],
        [(4, at(z, far_x, y, core), None), (3, at(z, flip(x), y, core), None), (8, at(z, 3 - x, y, core), None)],
        [(5, at(z, x, y, 1 - core), None)],
        [(7, at(z, x, far_y, core), None), (6, at(z, x, flip(y), core), None), (9, at(z, x, 3 - y, core), None)],
    ]
    arrivals = [[0], [1], [2], [3, 4, 8], [5], [6, 7, 9]]

    def guarded(condition, action):
        if condition is None:
            action()
        else:
            pl.when(condition)(action)

    def greet(device):
        pl.semaphore_signal(barrier, inc=1, device_id=device, device_id_type=MESH)

    barrier = pltpu.get_barrier_semaphore()
    for stage in (0, 3, 4, 5):
        for _slot, device, _who in routes[stage]:
            greet(device)
    for stage in (1, 2):
        far, near = routes[stage]
        greet(near[1])
        guarded(far[2], lambda far=far: greet(far[1]))

    number = {}
    for stage in range(STAGES):
        for index in range(len(routes[stage])):
            number[stage, index] = len(number)

    def send(stage, index, c):
        slot, device, _who = routes[stage][index]
        return pltpu.make_async_remote_copy(
            src_ref=sent.at[stage, c],
            dst_ref=got.at[slot, c],
            send_sem=send_sem.at[number[stage, index]],
            recv_sem=recv_sem.at[slot, c],
            device_id=device,
            device_id_type=MESH,
        )

    def start_sends(stage, c):
        for index, (_slot, _device, who) in enumerate(routes[stage]):
            guarded(who, lambda index=index: send(stage, index, c).start())

    def receive(stage, c):
        for slot in arrivals[stage]:
            pltpu.make_async_remote_copy(
                src_ref=sent.at[stage, c],
                dst_ref=got.at[slot, c],
                send_sem=send_sem.at[0],
                recv_sem=recv_sem.at[slot, c],
                device_id=routes[stage][0][1],
                device_id_type=MESH,
            ).wait_recv()

    def widen(source, target):
        def step(i, carry):
            rows = source[pl.ds(i * 32, 32)].astype(F32).reshape(32 * H, D)
            target[pl.ds(pl.multiple_of(i * 32 * H, 32 * H), 32 * H), :] = rows
            return carry
        lax.fori_loop(0, T // 32, step, 0)

    def head_of(source, c):
        return source[pl.ds(c, T, stride=H), :].astype(BF16)

    copies[0].wait()
    widen(k_in, k32)
    copies[1].wait()
    widen(v_in, v32)
    wt[pl.ds(TILE, TILE), pl.ds(0, TILE)] = jnp.zeros((TILE, TILE), BF16)
    wt[pl.ds(3 * TILE, TILE), pl.ds(2 * TILE, TILE)] = jnp.zeros((TILE, TILE), BF16)

    waits = 10 + serves1.astype(jnp.int32) + serves2.astype(jnp.int32)
    pl.semaphore_wait(barrier, waits)

    lane = lax.rem(lax.broadcasted_iota(jnp.int32, (16, T), 1), TILE)
    group = lax.broadcasted_iota(jnp.int32, (16, T), 0)
    coarse = lax.shift_right_logical(lane, 3)
    coarse_diff = jnp.bitwise_xor(coarse, group)
    low_lane = lax.rem(lax.broadcasted_iota(jnp.int32, (8, T), 1), 8)
    low_row = lax.broadcasted_iota(jnp.int32, (8, T), 0)
    low_diff = jnp.bitwise_xor(low_lane, low_row)

    def gain(level, c):
        return lw[level, pl.ds(c, 1), :] * FACTOR[level]

    def local(c):
        q = head_of(q32, c)
        qh[c] = q
        keys = kh[c]
        wide = jnp.zeros((16, T), F32)
        for level in (4, 5, 6, 7):
            wide = jnp.where(coarse_diff >= (1 << (level - 4)), gain(level, c), wide)
        wide = jnp.where(coarse > group, wide, 0.0)
        narrow = jnp.broadcast_to(gain(0, c), (8, T))
        for level in (1, 2, 3):
            narrow = jnp.where(low_diff >= (1 << (level - 1)), gain(level, c), narrow)
        narrow = jnp.where(low_lane >= low_row, narrow, 0.0)
        gain8 = gain(8, c)
        gain9 = gain(9, c)
        shape3 = (16, 8, TILE)
        same = lax.shift_right_logical(lax.broadcasted_iota(jnp.int32, shape3, 2), 3) == lax.broadcasted_iota(
            jnp.int32, shape3, 0
        )
        for j in range(T // TILE):
            scores = dot_nt(keys[j * TILE:(j + 1) * TILE], q[j * TILE:])
            for i in range(j, T // TILE):
                cols = slice(i * TILE, (i + 1) * TILE)
                part = scores[:, (i - j) * TILE:(i - j + 1) * TILE]
                if i == j:
                    weight = jnp.where(
                        same,
                        jnp.broadcast_to(narrow[:, cols].reshape(1, 8, TILE), shape3),
                        jnp.broadcast_to(wide[:, cols].reshape(16, 1, TILE), shape3),
                    ).reshape(TILE, TILE)
                    part = part * weight
                elif i ^ j == 1:
                    part = part * gain8[:, cols]
                else:
                    part = part * gain9[:, cols]
                wt[pl.ds(j * TILE, TILE), pl.ds(i * TILE, TILE)] = part.astype(BF16)
        values = vt[c]
        half = T // 2
        acc[c, :, pl.ds(0, half)] = dot_nn(values[:, :half], wt[pl.ds(0, half), pl.ds(0, half)])
        acc[c, :, pl.ds(half, half)] = dot_nn(values, wt[:, pl.ds(half, half)])

    switches = [
        jnp.bitwise_and(lax.shift_right_logical(place, tier), 1).astype(F32) for tier in range(TIERS)
    ]

    def finish(c):
        half = T // 2
        buckets = [got[tier, c] for tier in range(TIERS - 1)]
        buckets.append((got[7, c].astype(F32) + got[9, c].astype(F32)).astype(BF16))
        for part in range(2):
            cols = pl.ds(part * half, half)
            q = qh[c, pl.ds(part * half, half), :]
            total = acc[c, :, cols]
            for tier in range(TIERS):
                row = lw[LOCAL_BITS + 1 + tier, pl.ds(c, 1), cols] * (
                    switches[tier] * FACTOR[LOCAL_BITS + 1 + tier]
                )
                total = total + dot_nt(buckets[tier], q) * row
            out[pl.ds(part * half * H + c, half, stride=H), :] = total.T

    def active(t, start):
        return jnp.logical_and(t >= start, t < start + H)

    def tick(t, carry):
        @pl.when(active(t, 0))
        def _():
            keys = head_of(k32, t)
            kh[t] = keys
            values = v32[pl.ds(t, T, stride=H), :].T.astype(BF16)
            vt[t] = values
            state = dot_nn(values, keys)
            run[t] = state
            sent[0, t] = state.astype(BF16)

        for stage in range(1, STAGES):
            @pl.when(active(t, DELAY[stage]))
            def _(stage=stage):
                c = t - DELAY[stage]
                receive(stage - 1, c)
                if stage == 4:
                    other = got[4, c].astype(F32) + got[8, c].astype(F32)
                    got[4, c] = other.astype(BF16)
                    total = run[c] + got[3, c].astype(F32) + other
                else:
                    total = run[c] + got[arrivals[stage - 1][0], c].astype(F32)
                run[c] = total
                sent[stage, c] = total.astype(BF16)

        for stage in range(STAGES):
            @pl.when(active(t, DELAY[stage]))
            def _(stage=stage):
                start_sends(stage, t - DELAY[stage])

        @pl.when(active(t, LOCAL_AT))
        def _():
            @pl.when(t == LOCAL_AT)
            def _():
                copies[2].wait()
                copies[3].wait()
                widen(x_in, q32)
            local(t - LOCAL_AT)

        @pl.when(active(t, DELAY[STAGES]))
        def _():
            c = t - DELAY[STAGES]
            receive(STAGES - 1, c)
            finish(c)

        return carry

    lax.fori_loop(0, TICKS, tick, 0)

    for stage in range(STAGES):
        for index, (slot, device, who) in enumerate(routes[stage]):
            whole = pltpu.make_async_remote_copy(
                src_ref=sent.at[stage],
                dst_ref=got.at[slot],
                send_sem=send_sem.at[number[stage, index]],
                recv_sem=recv_sem.at[slot, 0],
                device_id=device,
                device_id_type=MESH,
            )
            guarded(who, whole.wait_send)


def per_device(queries, key_vectors, value_vectors, level_weights):
    hbm = pl.BlockSpec(memory_space=pltpu.HBM)
    summed = pl.pallas_call(
        kernel,
        out_shape=pltpu.VMEM((T * H, D), F32),
        in_specs=[hbm] * 4,
        out_specs=pl.BlockSpec(memory_space=pltpu.VMEM),
        scratch_shapes=[
            pltpu.VMEM((T, H, D), BF16),
            pltpu.VMEM((T, H, D), BF16),
            pltpu.VMEM((T, H, D), BF16),
            pltpu.VMEM((LEVELS, H, T), F32),
            pltpu.VMEM((T * H, D), F32),
            pltpu.VMEM((T * H, D), F32),
            pltpu.VMEM((T * H, D), F32),
            pltpu.VMEM((H, T, D), BF16),
            pltpu.VMEM((H, T, D), BF16),
            pltpu.VMEM((H, D, T), BF16),
            pltpu.VMEM((T, T), BF16),
            pltpu.VMEM((H, D, T), F32),
            pltpu.VMEM((H, D, D), F32),
            pltpu.VMEM((STAGES, H, D, D), BF16),
            pltpu.VMEM((SLOTS, H, D, D), BF16),
            pltpu.SemaphoreType.DMA((4,)),
            pltpu.SemaphoreType.DMA((12,)),
            pltpu.SemaphoreType.DMA((SLOTS, H)),
        ],
        compiler_params=pltpu.CompilerParams(
            collective_id=0, has_side_effects=True, vmem_limit_bytes=62_400_000
        ),
    )(queries, key_vectors, value_vectors, level_weights)
    return summed.reshape(T, H, D).astype(BF16)


def solution(mesh):
    placed = (
        P(("outer", "inner"), None, None),
        P(("outer", "inner"), None, None),
        P(("outer", "inner"), None, None),
        P(None, None, ("outer", "inner")),
    )
    return jax.shard_map(
        per_device,
        mesh=mesh,
        in_specs=placed,
        out_specs=P(("outer", "inner"), None, None),
        check_vma=False,
    )
```

```python
import math

import jax
import jax.numpy as jnp
from jax import lax
from jax.experimental import pallas as pl
from jax.experimental.pallas import tpu as pltpu
from jax.sharding import PartitionSpec as P

MESH = pl.DeviceIdType.MESH
F32 = jnp.float32
BF16 = jnp.bfloat16

T = 512
H = 16
D = 128
TIERS = 8
LEVELS = 18
LOCAL_BITS = 9
TILE = 128
STAGES = 6
SLOTS = 10
DELAY = [0, 3, 6, 9, 12, 14, 17]
LOCAL_AT = 2
STRIP = 64
TICKS = H + DELAY[STAGES]
FACTOR = [2.0 ** (-0.5 * level) for level in range(LEVELS)]


def dot_nt(a, b):
    return lax.dot_general(a, b, (((1,), (1,)), ((), ())), preferred_element_type=F32)


def dot_nn(a, b):
    return lax.dot_general(a, b, (((1,), (0,)), ((), ())), preferred_element_type=F32)


def either(value, *options):
    found = value == options[0]
    for option in options[1:]:
        found = jnp.logical_or(found, value == option)
    return found


def kernel(
    q_hbm, k_hbm, v_hbm, lw_hbm, out,
    x_in, k_in, v_in, lw, qh, kh, vh, vt, wt, acc, heads,
    run, sent, got, in_sem, key_sem, value_sem, send_sem, recv_sem,
):
    outer = lax.axis_index("outer")
    inner = lax.axis_index("inner")
    core = lax.rem(outer, 2)
    y = lax.div(outer, 2)
    z = lax.rem(inner, 8)
    x = lax.div(inner, 8)
    p = lax.rem(z, 4)
    place = outer * 32 + inner

    def strip(i):
        return pl.ds(pl.multiple_of(i * STRIP, STRIP), STRIP)

    def key_copy(i):
        return pltpu.make_async_copy(k_hbm.at[strip(i)], k_in.at[strip(i)], key_sem.at[i])

    def value_copy(i):
        return pltpu.make_async_copy(v_hbm.at[strip(i)], v_in.at[strip(i)], value_sem.at[i])

    copies = [
        pltpu.make_async_copy(lw_hbm, lw, in_sem.at[0]),
        pltpu.make_async_copy(q_hbm, x_in, in_sem.at[1]),
    ]
    for i in range(T // STRIP):
        key_copy(i).start()
        value_copy(i).start()
    for copy in copies:
        copy.start()

    def flip(value):
        return value + 1 - 2 * lax.rem(value, 2)

    def at(zz, xx, yy, cc):
        return (yy * 2 + cc, xx * 8 + zz)

    base4 = z - p
    source1 = base4 + jnp.where(p < 2, 2, 1)
    second1 = base4 + jnp.where(p == 1, 3, 0)
    serves1 = either(p, 1, 2)
    source2 = jnp.where(either(z, 0, 1), 7, jnp.where(either(z, 6, 7), 0, jnp.where(either(z, 2, 3), 4, 3)))
    second2 = jnp.where(z == 0, 6, jnp.where(z == 7, 1, jnp.where(z == 3, 5, 2)))
    serves2 = either(z, 0, 3, 4, 7)

    far_y = lax.rem(y + 2, 4)
    low_y = y < 2
    even_y = lax.rem(y, 2) == 0
    taken = {6: jnp.logical_not(even_y), 7: jnp.logical_not(low_y), 9: jnp.logical_not(low_y)}
    far_x = lax.rem(x + 2, 4)
    routes = [
        [(0, at(flip(z), x, y, core), None)],
        [(1, at(second1, x, y, core), serves1), (1, at(source1, x, y, core), serves1)],
        [(2, at(second2, x, y, core), serves2), (2, at(source2, x, y, core), serves2)],
        [(4, at(z, far_x, y, core), None), (3, at(z, flip(x), y, core), None), (8, at(z, 3 - x, y, core), None)],
        [(5, at(z, x, y, 1 - core), None)],
        [(7, at(z, x, far_y, core), low_y), (6, at(z, x, flip(y), core), even_y), (9, at(z, x, 3 - y, core), low_y)],
    ]
    arrivals = [[0], [1], [2], [3, 4, 8], [5], [6, 7, 9]]

    def guarded(condition, action):
        if condition is None:
            action()
        else:
            pl.when(condition)(action)

    def greet(device):
        pl.semaphore_signal(barrier, inc=1, device_id=device, device_id_type=MESH)

    barrier = pltpu.get_barrier_semaphore()
    for stage in (0, 3, 4, 5):
        for _slot, device, _who in routes[stage]:
            greet(device)
    for stage in (1, 2):
        far, near = routes[stage]
        greet(near[1])
        guarded(far[2], lambda far=far: greet(far[1]))

    number = {}
    for stage in range(STAGES):
        for index in range(len(routes[stage])):
            number[stage, index] = len(number)

    def send(stage, index, c):
        slot, device, _who = routes[stage][index]
        return pltpu.make_async_remote_copy(
            src_ref=sent.at[stage, c],
            dst_ref=got.at[slot, c],
            send_sem=send_sem.at[number[stage, index]],
            recv_sem=recv_sem.at[slot, c],
            device_id=device,
            device_id_type=MESH,
        )

    def start_sends(stage, c):
        for index, (_slot, _device, who) in enumerate(routes[stage]):
            guarded(who, lambda index=index: send(stage, index, c).start())

    def receive(stage, c):
        for slot in arrivals[stage]:
            copy = pltpu.make_async_remote_copy(
                src_ref=sent.at[stage, c],
                dst_ref=got.at[slot, c],
                send_sem=send_sem.at[0],
                recv_sem=recv_sem.at[slot, c],
                device_id=routes[stage][0][1],
                device_id_type=MESH,
            )
            guarded(taken.get(slot), copy.wait_recv)

    def by_head(source, target, i):
        target[:, strip(i), :] = jnp.transpose(source[strip(i)], (1, 0, 2))

    def unpack_keys_values(i, carry):
        key_copy(i).wait()
        by_head(k_in, kh, i)
        value_copy(i).wait()
        by_head(v_in, vh, i)
        return carry

    def unpack_queries(i, carry):
        by_head(x_in, qh, i)
        return carry

    lax.fori_loop(0, T // STRIP, unpack_keys_values, 0)
    for slot, who in taken.items():
        @pl.when(jnp.logical_not(who))
        def _(slot=slot):
            got[slot] = jnp.zeros((H, D, D), BF16)
    wt[pl.ds(TILE, TILE), pl.ds(0, TILE)] = jnp.zeros((TILE, TILE), BF16)
    wt[pl.ds(3 * TILE, TILE), pl.ds(2 * TILE, TILE)] = jnp.zeros((TILE, TILE), BF16)

    waits = 10 + serves1.astype(jnp.int32) + serves2.astype(jnp.int32)
    pl.semaphore_wait(barrier, waits)

    lane = lax.rem(lax.broadcasted_iota(jnp.int32, (16, T), 1), TILE)
    group = lax.broadcasted_iota(jnp.int32, (16, T), 0)
    coarse = lax.shift_right_logical(lane, 3)
    coarse_diff = jnp.bitwise_xor(coarse, group)
    low_lane = lax.rem(lax.broadcasted_iota(jnp.int32, (8, T), 1), 8)
    low_row = lax.broadcasted_iota(jnp.int32, (8, T), 0)
    low_diff = jnp.bitwise_xor(low_lane, low_row)

    def gain(level, c):
        return lw[level, pl.ds(c, 1), :] * FACTOR[level]

    def local(c):
        q = qh[c]
        keys = kh[c]
        wide = jnp.zeros((16, T), F32)
        for level in (4, 5, 6, 7):
            wide = jnp.where(coarse_diff >= (1 << (level - 4)), gain(level, c), wide)
        wide = jnp.where(coarse > group, wide, 0.0)
        narrow = jnp.broadcast_to(gain(0, c), (8, T))
        for level in (1, 2, 3):
            narrow = jnp.where(low_diff >= (1 << (level - 1)), gain(level, c), narrow)
        narrow = jnp.where(low_lane >= low_row, narrow, 0.0)
        gain8 = gain(8, c)
        gain9 = gain(9, c)
        shape3 = (16, 8, TILE)
        same = lax.shift_right_logical(lax.broadcasted_iota(jnp.int32, shape3, 2), 3) == lax.broadcasted_iota(
            jnp.int32, shape3, 0
        )
        for j in range(T // TILE):
            scores = dot_nt(keys[j * TILE:(j + 1) * TILE], q[j * TILE:])
            for i in range(j, T // TILE):
                cols = slice(i * TILE, (i + 1) * TILE)
                part = scores[:, (i - j) * TILE:(i - j + 1) * TILE]
                if i == j:
                    weight = jnp.where(
                        same,
                        jnp.broadcast_to(narrow[:, cols].reshape(1, 8, TILE), shape3),
                        jnp.broadcast_to(wide[:, cols].reshape(16, 1, TILE), shape3),
                    ).reshape(TILE, TILE)
                    part = part * weight
                elif i ^ j == 1:
                    part = part * gain8[:, cols]
                else:
                    part = part * gain9[:, cols]
                wt[pl.ds(j * TILE, TILE), pl.ds(i * TILE, TILE)] = part.astype(BF16)
        values = vt[c]
        half = T // 2
        acc[c, :, pl.ds(0, half)] = dot_nn(values[:, :half], wt[pl.ds(0, half), pl.ds(0, half)])
        acc[c, :, pl.ds(half, half)] = dot_nn(values, wt[:, pl.ds(half, half)])

    switches = [
        jnp.bitwise_and(lax.shift_right_logical(place, tier), 1).astype(F32) for tier in range(TIERS)
    ]

    def finish(c):
        half = T // 2
        buckets = [got[tier, c] for tier in range(TIERS - 1)]
        buckets.append((got[7, c].astype(F32) + got[9, c].astype(F32)).astype(BF16))
        for part in range(2):
            cols = pl.ds(part * half, half)
            q = qh[c, pl.ds(part * half, half), :]
            total = acc[c, :, cols]
            for tier in range(TIERS):
                row = lw[LOCAL_BITS + 1 + tier, pl.ds(c, 1), cols] * (
                    switches[tier] * FACTOR[LOCAL_BITS + 1 + tier]
                )
                total = total + dot_nt(buckets[tier], q) * row
            heads[c, pl.ds(part * half, half), :] = total.astype(BF16).T

    def active(t, start):
        return jnp.logical_and(t >= start, t < start + H)

    def tick(t, carry):
        @pl.when(active(t, 0))
        def _():
            values = vh[t].T
            vt[t] = values
            state = dot_nn(values, kh[t])
            run[t] = state
            sent[0, t] = state.astype(BF16)

        for stage in reversed(range(1, STAGES)):
            @pl.when(active(t, DELAY[stage]))
            def _(stage=stage):
                c = t - DELAY[stage]
                receive(stage - 1, c)
                if stage == 4:
                    other = got[4, c].astype(F32) + got[8, c].astype(F32)
                    got[4, c] = other.astype(BF16)
                    total = run[c] + got[3, c].astype(F32) + other
                else:
                    total = run[c] + got[arrivals[stage - 1][0], c].astype(F32)
                run[c] = total
                sent[stage, c] = total.astype(BF16)

        for stage in (4, 5, 3, 2, 1, 0):
            @pl.when(active(t, DELAY[stage]))
            def _(stage=stage):
                start_sends(stage, t - DELAY[stage])

        @pl.when(active(t, LOCAL_AT))
        def _():
            @pl.when(t == LOCAL_AT)
            def _():
                copies[0].wait()
                copies[1].wait()
                lax.fori_loop(0, T // STRIP, unpack_queries, 0)
            local(t - LOCAL_AT)

        @pl.when(active(t, DELAY[STAGES]))
        def _():
            c = t - DELAY[STAGES]
            receive(STAGES - 1, c)
            finish(c)

        return carry

    lax.fori_loop(0, TICKS, tick, 0)

    def by_position(i, carry):
        out[strip(i)] = jnp.transpose(heads[:, strip(i), :], (1, 0, 2))
        return carry

    lax.fori_loop(0, T // STRIP, by_position, 0)

    for stage in range(STAGES):
        for index, (slot, device, who) in enumerate(routes[stage]):
            whole = pltpu.make_async_remote_copy(
                src_ref=sent.at[stage],
                dst_ref=got.at[slot],
                send_sem=send_sem.at[number[stage, index]],
                recv_sem=recv_sem.at[slot, 0],
                device_id=device,
                device_id_type=MESH,
            )
            guarded(who, whole.wait_send)


def per_device(queries, key_vectors, value_vectors, level_weights):
    hbm = pl.BlockSpec(memory_space=pltpu.HBM)
    return pl.pallas_call(
        kernel,
        out_shape=pltpu.VMEM((T, H, D), BF16),
        in_specs=[hbm] * 4,
        out_specs=pl.BlockSpec(memory_space=pltpu.VMEM),
        scratch_shapes=[
            pltpu.VMEM((T, H, D), BF16),
            pltpu.VMEM((T, H, D), BF16),
            pltpu.VMEM((T, H, D), BF16),
            pltpu.VMEM((LEVELS, H, T), F32),
            pltpu.VMEM((H, T, D), BF16),
            pltpu.VMEM((H, T, D), BF16),
            pltpu.VMEM((H, T, D), BF16),
            pltpu.VMEM((H, D, T), BF16),
            pltpu.VMEM((T, T), BF16),
            pltpu.VMEM((H, D, T), F32),
            pltpu.VMEM((H, T, D), BF16),
            pltpu.VMEM((H, D, D), F32),
            pltpu.VMEM((STAGES, H, D, D), BF16),
            pltpu.VMEM((SLOTS, H, D, D), BF16),
            pltpu.SemaphoreType.DMA((2,)),
            pltpu.SemaphoreType.DMA((T // STRIP,)),
            pltpu.SemaphoreType.DMA((T // STRIP,)),
            pltpu.SemaphoreType.DMA((12,)),
            pltpu.SemaphoreType.DMA((SLOTS, H)),
        ],
        compiler_params=pltpu.CompilerParams(
            collective_id=0, has_side_effects=True, vmem_limit_bytes=64_500_000
        ),
    )(queries, key_vectors, value_vectors, level_weights)


def solution(mesh):
    placed = (
        P(("outer", "inner"), None, None),
        P(("outer", "inner"), None, None),
        P(("outer", "inner"), None, None),
        P(None, None, ("outer", "inner")),
    )
    return jax.shard_map(
        per_device,
        mesh=mesh,
        in_specs=placed,
        out_specs=P(("outer", "inner"), None, None),
        check_vma=False,
    )
```

```python
import math

import jax
import jax.numpy as jnp
from jax import lax
from jax.experimental import pallas as pl
from jax.experimental.pallas import tpu as pltpu
from jax.sharding import PartitionSpec as P

MESH = pl.DeviceIdType.MESH
F32 = jnp.float32
BF16 = jnp.bfloat16

T = 512
H = 16
D = 128
TIERS = 8
LEVELS = 18
LOCAL_BITS = 9
TILE = 128
STAGES = 6
SLOTS = 10
DELAY = [0, 3, 6, 9, 12, 13, 16]
LOCAL_AT = 3
STRIP = 64
HALF = 8
TICKS = H + DELAY[STAGES]
FACTOR = [2.0 ** (-0.5 * level) for level in range(LEVELS)]


def dot_nt(a, b):
    return lax.dot_general(a, b, (((1,), (1,)), ((), ())), preferred_element_type=F32)


def dot_nn(a, b):
    return lax.dot_general(a, b, (((1,), (0,)), ((), ())), preferred_element_type=F32)


def either(value, *options):
    found = value == options[0]
    for option in options[1:]:
        found = jnp.logical_or(found, value == option)
    return found


def kernel(
    q_hbm, k_hbm, v_hbm, lw_hbm, out,
    x_in, k_in, v_in, lw, qh, kh, vh, vt, wt, acc, heads,
    run, sent, got, in_sem, key_sem, value_sem, send_sem, recv_sem,
):
    outer = lax.axis_index("outer")
    inner = lax.axis_index("inner")
    core = lax.rem(outer, 2)
    y = lax.div(outer, 2)
    z = lax.rem(inner, 8)
    x = lax.div(inner, 8)
    p = lax.rem(z, 4)
    place = outer * 32 + inner

    def strip(i):
        return pl.ds(pl.multiple_of(i * STRIP, STRIP), STRIP)

    def key_copy(i):
        return pltpu.make_async_copy(k_hbm.at[strip(i)], k_in.at[strip(i)], key_sem.at[i])

    def value_copy(i):
        return pltpu.make_async_copy(v_hbm.at[strip(i)], v_in.at[strip(i)], value_sem.at[i])

    copies = [
        pltpu.make_async_copy(lw_hbm, lw, in_sem.at[0]),
        pltpu.make_async_copy(q_hbm, x_in, in_sem.at[1]),
    ]
    for i in range(T // STRIP):
        key_copy(i).start()
        value_copy(i).start()

    def flip(value):
        return value + 1 - 2 * lax.rem(value, 2)

    def at(zz, xx, yy, cc):
        return (yy * 2 + cc, xx * 8 + zz)

    base4 = z - p
    source1 = base4 + jnp.where(p < 2, 2, 1)
    second1 = base4 + jnp.where(p == 1, 3, 0)
    serves1 = either(p, 1, 2)
    source2 = jnp.where(either(z, 0, 1), 7, jnp.where(either(z, 6, 7), 0, jnp.where(either(z, 2, 3), 4, 3)))
    second2 = jnp.where(z == 0, 6, jnp.where(z == 7, 1, jnp.where(z == 3, 5, 2)))
    serves2 = either(z, 0, 3, 4, 7)

    far_y = lax.rem(y + 2, 4)
    low_y = y < 2
    even_y = lax.rem(y, 2) == 0
    taken = {6: jnp.logical_not(even_y), 7: jnp.logical_not(low_y), 9: jnp.logical_not(low_y)}
    far_x = lax.rem(x + 2, 4)
    routes = [
        [(0, at(flip(z), x, y, core), None)],
        [(1, at(second1, x, y, core), serves1), (1, at(source1, x, y, core), serves1)],
        [(2, at(second2, x, y, core), serves2), (2, at(source2, x, y, core), serves2)],
        [(4, at(z, far_x, y, core), None), (3, at(z, flip(x), y, core), None), (8, at(z, 3 - x, y, core), None)],
        [(5, at(z, x, y, 1 - core), None)],
        [(7, at(z, x, far_y, core), low_y), (6, at(z, x, flip(y), core), even_y), (9, at(z, x, 3 - y, core), low_y)],
    ]
    arrivals = [[0], [1], [2], [3, 4, 8], [5], [6, 7, 9]]

    def guarded(condition, action):
        if condition is None:
            action()
        else:
            pl.when(condition)(action)

    def greet(device):
        pl.semaphore_signal(barrier, inc=1, device_id=device, device_id_type=MESH)

    barrier = pltpu.get_barrier_semaphore()
    for stage in (0, 3, 4, 5):
        for _slot, device, _who in routes[stage]:
            greet(device)
    for stage in (1, 2):
        far, near = routes[stage]
        greet(near[1])
        guarded(far[2], lambda far=far: greet(far[1]))

    number = {}
    for stage in range(STAGES):
        for index in range(len(routes[stage])):
            number[stage, index] = len(number)

    def send(stage, index, c):
        slot, device, _who = routes[stage][index]
        return pltpu.make_async_remote_copy(
            src_ref=sent.at[stage, c],
            dst_ref=got.at[slot, c],
            send_sem=send_sem.at[number[stage, index]],
            recv_sem=recv_sem.at[slot, c],
            device_id=device,
            device_id_type=MESH,
        )

    def start_sends(stage, c):
        for index, (_slot, _device, who) in enumerate(routes[stage]):
            guarded(who, lambda index=index: send(stage, index, c).start())

    def receive(stage, c):
        for slot in arrivals[stage]:
            copy = pltpu.make_async_remote_copy(
                src_ref=sent.at[stage, c],
                dst_ref=got.at[slot, c],
                send_sem=send_sem.at[0],
                recv_sem=recv_sem.at[slot, c],
                device_id=routes[stage][0][1],
                device_id_type=MESH,
            )
            guarded(taken.get(slot), copy.wait_recv)

    def by_head(source, target, i):
        target[:, strip(i), :] = jnp.transpose(source[strip(i)], (1, 0, 2))

    def unpack_keys_values(i, carry):
        key_copy(i).wait()
        by_head(k_in, kh, i)
        value_copy(i).wait()
        by_head(v_in, vh, i)
        return carry

    def unpack_queries(i, carry):
        by_head(x_in, qh, i)
        return carry

    lax.fori_loop(0, T // STRIP, unpack_keys_values, 0)
    for copy in copies:
        copy.start()
    for slot, who in taken.items():
        @pl.when(jnp.logical_not(who))
        def _(slot=slot):
            got[slot] = jnp.zeros((H, D, D), BF16)
    wt[pl.ds(TILE, TILE), pl.ds(0, TILE)] = jnp.zeros((TILE, TILE), BF16)
    wt[pl.ds(3 * TILE, TILE), pl.ds(2 * TILE, TILE)] = jnp.zeros((TILE, TILE), BF16)

    waits = 10 + serves1.astype(jnp.int32) + serves2.astype(jnp.int32)
    pl.semaphore_wait(barrier, waits)

    lane = lax.rem(lax.broadcasted_iota(jnp.int32, (16, T), 1), TILE)
    group = lax.broadcasted_iota(jnp.int32, (16, T), 0)
    coarse = lax.shift_right_logical(lane, 3)
    coarse_diff = jnp.bitwise_xor(coarse, group)
    low_lane = lax.rem(lax.broadcasted_iota(jnp.int32, (8, T), 1), 8)
    low_row = lax.broadcasted_iota(jnp.int32, (8, T), 0)
    low_diff = jnp.bitwise_xor(low_lane, low_row)

    def gain(level, c):
        return lw[level, pl.ds(c, 1), :] * FACTOR[level]

    def local(c):
        q = qh[c]
        keys = kh[c]
        wide = jnp.zeros((16, T), F32)
        for level in (4, 5, 6, 7):
            wide = jnp.where(coarse_diff >= (1 << (level - 4)), gain(level, c), wide)
        wide = jnp.where(coarse > group, wide, 0.0)
        narrow = jnp.broadcast_to(gain(0, c), (8, T))
        for level in (1, 2, 3):
            narrow = jnp.where(low_diff >= (1 << (level - 1)), gain(level, c), narrow)
        narrow = jnp.where(low_lane >= low_row, narrow, 0.0)
        gain8 = gain(8, c)
        gain9 = gain(9, c)
        shape3 = (16, 8, TILE)
        same = lax.shift_right_logical(lax.broadcasted_iota(jnp.int32, shape3, 2), 3) == lax.broadcasted_iota(
            jnp.int32, shape3, 0
        )
        for j in range(T // TILE):
            scores = dot_nt(keys[j * TILE:(j + 1) * TILE], q[j * TILE:])
            for i in range(j, T // TILE):
                cols = slice(i * TILE, (i + 1) * TILE)
                part = scores[:, (i - j) * TILE:(i - j + 1) * TILE]
                if i == j:
                    weight = jnp.where(
                        same,
                        jnp.broadcast_to(narrow[:, cols].reshape(1, 8, TILE), shape3),
                        jnp.broadcast_to(wide[:, cols].reshape(16, 1, TILE), shape3),
                    ).reshape(TILE, TILE)
                    part = part * weight
                elif i ^ j == 1:
                    part = part * gain8[:, cols]
                else:
                    part = part * gain9[:, cols]
                wt[pl.ds(j * TILE, TILE), pl.ds(i * TILE, TILE)] = part.astype(BF16)
        values = vt[c]
        half = T // 2
        acc[c, :, pl.ds(0, half)] = dot_nn(values[:, :half], wt[pl.ds(0, half), pl.ds(0, half)])
        acc[c, :, pl.ds(half, half)] = dot_nn(values, wt[:, pl.ds(half, half)])

    switches = [
        jnp.bitwise_and(lax.shift_right_logical(place, tier), 1).astype(F32) for tier in range(TIERS)
    ]

    def finish(c):
        half = T // 2
        buckets = [got[tier, c] for tier in range(TIERS - 1)]
        buckets.append((got[7, c].astype(F32) + got[9, c].astype(F32)).astype(BF16))
        for part in range(2):
            cols = pl.ds(part * half, half)
            q = qh[c, pl.ds(part * half, half), :]
            total = acc[c, :, cols]
            for tier in range(TIERS):
                row = lw[LOCAL_BITS + 1 + tier, pl.ds(c, 1), cols] * (
                    switches[tier] * FACTOR[LOCAL_BITS + 1 + tier]
                )
                total = total + dot_nt(buckets[tier], q) * row
            heads[c, pl.ds(part * half, half), :] = total.astype(BF16).T

    def active(t, start):
        return jnp.logical_and(t >= start, t < start + H)

    def by_position(half):
        some = pl.ds(half * HALF, HALF)

        def step(i, carry):
            out[strip(i), some, :] = jnp.transpose(heads[some, strip(i), :], (1, 0, 2))
            return carry

        lax.fori_loop(0, T // STRIP, step, 0)

    def tick(t, carry):
        @pl.when(active(t, 0))
        def _():
            values = vh[t].T
            vt[t] = values
            state = dot_nn(values, kh[t])
            run[t] = state
            sent[0, t] = state.astype(BF16)

        for stage in reversed(range(1, STAGES)):
            @pl.when(active(t, DELAY[stage]))
            def _(stage=stage):
                c = t - DELAY[stage]
                receive(stage - 1, c)
                if stage == 4:
                    other = got[4, c].astype(F32) + got[8, c].astype(F32)
                    got[4, c] = other.astype(BF16)
                    total = run[c] + got[3, c].astype(F32) + other
                else:
                    total = run[c] + got[arrivals[stage - 1][0], c].astype(F32)
                run[c] = total
                sent[stage, c] = total.astype(BF16)

        for stage in (4, 5, 3, 2, 1, 0):
            @pl.when(active(t, DELAY[stage]))
            def _(stage=stage):
                start_sends(stage, t - DELAY[stage])

        @pl.when(active(t, LOCAL_AT))
        def _():
            @pl.when(t == LOCAL_AT)
            def _():
                copies[0].wait()
                copies[1].wait()
                lax.fori_loop(0, T // STRIP, unpack_queries, 0)
            local(t - LOCAL_AT)

        @pl.when(active(t, DELAY[STAGES]))
        def _():
            c = t - DELAY[STAGES]
            receive(STAGES - 1, c)
            finish(c)

        @pl.when(t == DELAY[STAGES] + HALF)
        def _():
            by_position(0)

        return carry

    lax.fori_loop(0, TICKS, tick, 0)

    by_position(1)

    for stage in range(STAGES):
        for index, (slot, device, who) in enumerate(routes[stage]):
            whole = pltpu.make_async_remote_copy(
                src_ref=sent.at[stage],
                dst_ref=got.at[slot],
                send_sem=send_sem.at[number[stage, index]],
                recv_sem=recv_sem.at[slot, 0],
                device_id=device,
                device_id_type=MESH,
            )
            guarded(who, whole.wait_send)


def per_device(queries, key_vectors, value_vectors, level_weights):
    hbm = pl.BlockSpec(memory_space=pltpu.HBM)
    return pl.pallas_call(
        kernel,
        out_shape=pltpu.VMEM((T, H, D), BF16),
        in_specs=[hbm] * 4,
        out_specs=pl.BlockSpec(memory_space=pltpu.VMEM),
        scratch_shapes=[
            pltpu.VMEM((T, H, D), BF16),
            pltpu.VMEM((T, H, D), BF16),
            pltpu.VMEM((T, H, D), BF16),
            pltpu.VMEM((LEVELS, H, T), F32),
            pltpu.VMEM((H, T, D), BF16),
            pltpu.VMEM((H, T, D), BF16),
            pltpu.VMEM((H, T, D), BF16),
            pltpu.VMEM((H, D, T), BF16),
            pltpu.VMEM((T, T), BF16),
            pltpu.VMEM((H, D, T), F32),
            pltpu.VMEM((H, T, D), BF16),
            pltpu.VMEM((H, D, D), F32),
            pltpu.VMEM((STAGES, H, D, D), BF16),
            pltpu.VMEM((SLOTS, H, D, D), BF16),
            pltpu.SemaphoreType.DMA((2,)),
            pltpu.SemaphoreType.DMA((T // STRIP,)),
            pltpu.SemaphoreType.DMA((T // STRIP,)),
            pltpu.SemaphoreType.DMA((12,)),
            pltpu.SemaphoreType.DMA((SLOTS, H)),
        ],
        compiler_params=pltpu.CompilerParams(
            collective_id=0, has_side_effects=True, vmem_limit_bytes=64_500_000
        ),
    )(queries, key_vectors, value_vectors, level_weights)


def solution(mesh):
    placed = (
        P(("outer", "inner"), None, None),
        P(("outer", "inner"), None, None),
        P(("outer", "inner"), None, None),
        P(None, None, ("outer", "inner")),
    )
    return jax.shard_map(
        per_device,
        mesh=mesh,
        in_specs=placed,
        out_specs=P(("outer", "inner"), None, None),
        check_vma=False,
    )
```

```python
import math

import jax
import jax.numpy as jnp
from jax import lax
from jax.experimental import pallas as pl
from jax.experimental.pallas import tpu as pltpu
from jax.sharding import PartitionSpec as P

MESH = pl.DeviceIdType.MESH
F32 = jnp.float32
BF16 = jnp.bfloat16

T = 512
H = 16
D = 128
TIERS = 8
LEVELS = 18
LOCAL_BITS = 9
TILE = 128
STAGES = 6
SLOTS = 10
DELAY = [0, 3, 6, 10, 13, 14, 17]
LOCAL_AT = 3
STRIP = 64
HALF = 8
TICKS = H + DELAY[STAGES]
FACTOR = [2.0 ** (-0.5 * level) for level in range(LEVELS)]


def dot_nt(a, b):
    return lax.dot_general(a, b, (((1,), (1,)), ((), ())), preferred_element_type=F32)


def dot_nn(a, b):
    return lax.dot_general(a, b, (((1,), (0,)), ((), ())), preferred_element_type=F32)


def either(value, *options):
    found = value == options[0]
    for option in options[1:]:
        found = jnp.logical_or(found, value == option)
    return found


def kernel(
    q_hbm, k_hbm, v_hbm, lw_hbm, out,
    x_in, k_in, v_in, lw, qh, kh, vh, vt, wt, acc, heads,
    run, sent, got, in_sem, key_sem, value_sem, send_sem, recv_sem,
):
    outer = lax.axis_index("outer")
    inner = lax.axis_index("inner")
    core = lax.rem(outer, 2)
    y = lax.div(outer, 2)
    z = lax.rem(inner, 8)
    x = lax.div(inner, 8)
    p = lax.rem(z, 4)
    place = outer * 32 + inner

    def strip(i):
        return pl.ds(pl.multiple_of(i * STRIP, STRIP), STRIP)

    def key_copy(i):
        return pltpu.make_async_copy(k_hbm.at[strip(i)], k_in.at[strip(i)], key_sem.at[i])

    def value_copy(i):
        return pltpu.make_async_copy(v_hbm.at[strip(i)], v_in.at[strip(i)], value_sem.at[i])

    copies = [
        pltpu.make_async_copy(lw_hbm, lw, in_sem.at[0]),
        pltpu.make_async_copy(q_hbm, x_in, in_sem.at[1]),
    ]
    for i in range(T // STRIP):
        key_copy(i).start()
        value_copy(i).start()

    def flip(value):
        return value + 1 - 2 * lax.rem(value, 2)

    def at(zz, xx, yy, cc):
        return (yy * 2 + cc, xx * 8 + zz)

    base4 = z - p
    source1 = base4 + jnp.where(p < 2, 2, 1)
    second1 = base4 + jnp.where(p == 1, 3, 0)
    serves1 = either(p, 1, 2)
    source2 = jnp.where(either(z, 0, 1), 7, jnp.where(either(z, 6, 7), 0, jnp.where(either(z, 2, 3), 4, 3)))
    second2 = jnp.where(z == 0, 6, jnp.where(z == 7, 1, jnp.where(z == 3, 5, 2)))
    serves2 = either(z, 0, 3, 4, 7)

    far_y = lax.rem(y + 2, 4)
    low_y = y < 2
    even_y = lax.rem(y, 2) == 0
    taken = {6: jnp.logical_not(even_y), 7: jnp.logical_not(low_y), 9: jnp.logical_not(low_y)}
    far_x = lax.rem(x + 2, 4)
    routes = [
        [(0, at(flip(z), x, y, core), None)],
        [(1, at(second1, x, y, core), serves1), (1, at(source1, x, y, core), serves1)],
        [(2, at(second2, x, y, core), serves2), (2, at(source2, x, y, core), serves2)],
        [(4, at(z, far_x, y, core), None), (3, at(z, flip(x), y, core), None), (8, at(z, 3 - x, y, core), None)],
        [(5, at(z, x, y, 1 - core), None)],
        [(7, at(z, x, far_y, core), low_y), (6, at(z, x, flip(y), core), even_y), (9, at(z, x, 3 - y, core), low_y)],
    ]
    arrivals = [[0], [1], [2], [3, 4, 8], [5], [6, 7, 9]]

    def guarded(condition, action):
        if condition is None:
            action()
        else:
            pl.when(condition)(action)

    def greet(device):
        pl.semaphore_signal(barrier, inc=1, device_id=device, device_id_type=MESH)

    barrier = pltpu.get_barrier_semaphore()
    for stage in (0, 3, 4, 5):
        for _slot, device, _who in routes[stage]:
            greet(device)
    for stage in (1, 2):
        far, near = routes[stage]
        greet(near[1])
        guarded(far[2], lambda far=far: greet(far[1]))

    number = {}
    for stage in range(STAGES):
        for index in range(len(routes[stage])):
            number[stage, index] = len(number)

    def send(stage, index, c):
        slot, device, _who = routes[stage][index]
        return pltpu.make_async_remote_copy(
            src_ref=sent.at[stage, c],
            dst_ref=got.at[slot, c],
            send_sem=send_sem.at[number[stage, index]],
            recv_sem=recv_sem.at[slot, c],
            device_id=device,
            device_id_type=MESH,
        )

    def start_sends(stage, c):
        for index, (_slot, _device, who) in enumerate(routes[stage]):
            guarded(who, lambda index=index: send(stage, index, c).start())

    def receive(stage, c):
        for slot in arrivals[stage]:
            copy = pltpu.make_async_remote_copy(
                src_ref=sent.at[stage, c],
                dst_ref=got.at[slot, c],
                send_sem=send_sem.at[0],
                recv_sem=recv_sem.at[slot, c],
                device_id=routes[stage][0][1],
                device_id_type=MESH,
            )
            guarded(taken.get(slot), copy.wait_recv)

    def by_head(source, target, i):
        target[:, strip(i), :] = jnp.transpose(source[strip(i)], (1, 0, 2))

    def unpack_keys_values(i, carry):
        key_copy(i).wait()
        by_head(k_in, kh, i)
        value_copy(i).wait()
        by_head(v_in, vh, i)
        return carry

    def unpack_queries(i, carry):
        by_head(x_in, qh, i)
        return carry

    lax.fori_loop(0, T // STRIP, unpack_keys_values, 0)
    for copy in copies:
        copy.start()
    for slot, who in taken.items():
        @pl.when(jnp.logical_not(who))
        def _(slot=slot):
            got[slot] = jnp.zeros((H, D, D), BF16)
    wt[pl.ds(TILE, TILE), pl.ds(0, TILE)] = jnp.zeros((TILE, TILE), BF16)
    wt[pl.ds(3 * TILE, TILE), pl.ds(2 * TILE, TILE)] = jnp.zeros((TILE, TILE), BF16)

    waits = 10 + serves1.astype(jnp.int32) + serves2.astype(jnp.int32)
    pl.semaphore_wait(barrier, waits)

    lane = lax.rem(lax.broadcasted_iota(jnp.int32, (16, T), 1), TILE)
    group = lax.broadcasted_iota(jnp.int32, (16, T), 0)
    coarse = lax.shift_right_logical(lane, 3)
    coarse_diff = jnp.bitwise_xor(coarse, group)
    low_lane = lax.rem(lax.broadcasted_iota(jnp.int32, (8, T), 1), 8)
    low_row = lax.broadcasted_iota(jnp.int32, (8, T), 0)
    low_diff = jnp.bitwise_xor(low_lane, low_row)

    def gain(level, c):
        return lw[level, pl.ds(c, 1), :] * FACTOR[level]

    def local(c):
        q = qh[c]
        keys = kh[c]
        wide = jnp.zeros((16, T), F32)
        for level in (4, 5, 6, 7):
            wide = jnp.where(coarse_diff >= (1 << (level - 4)), gain(level, c), wide)
        wide = jnp.where(coarse > group, wide, 0.0)
        narrow = jnp.broadcast_to(gain(0, c), (8, T))
        for level in (1, 2, 3):
            narrow = jnp.where(low_diff >= (1 << (level - 1)), gain(level, c), narrow)
        narrow = jnp.where(low_lane >= low_row, narrow, 0.0)
        gain8 = gain(8, c)
        gain9 = gain(9, c)
        shape3 = (16, 8, TILE)
        same = lax.shift_right_logical(lax.broadcasted_iota(jnp.int32, shape3, 2), 3) == lax.broadcasted_iota(
            jnp.int32, shape3, 0
        )
        for j in range(T // TILE):
            scores = dot_nt(keys[j * TILE:(j + 1) * TILE], q[j * TILE:])
            for i in range(j, T // TILE):
                cols = slice(i * TILE, (i + 1) * TILE)
                part = scores[:, (i - j) * TILE:(i - j + 1) * TILE]
                if i == j:
                    weight = jnp.where(
                        same,
                        jnp.broadcast_to(narrow[:, cols].reshape(1, 8, TILE), shape3),
                        jnp.broadcast_to(wide[:, cols].reshape(16, 1, TILE), shape3),
                    ).reshape(TILE, TILE)
                    part = part * weight
                elif i ^ j == 1:
                    part = part * gain8[:, cols]
                else:
                    part = part * gain9[:, cols]
                wt[pl.ds(j * TILE, TILE), pl.ds(i * TILE, TILE)] = part.astype(BF16)
        values = vt[c]
        half = T // 2
        acc[c, :, pl.ds(0, half)] = dot_nn(values[:, :half], wt[pl.ds(0, half), pl.ds(0, half)])
        acc[c, :, pl.ds(half, half)] = dot_nn(values, wt[:, pl.ds(half, half)])

    switches = [
        jnp.bitwise_and(lax.shift_right_logical(place, tier), 1).astype(F32) for tier in range(TIERS)
    ]

    def finish(c):
        half = T // 2
        buckets = [got[tier, c] for tier in range(TIERS - 1)]
        buckets.append((got[7, c].astype(F32) + got[9, c].astype(F32)).astype(BF16))
        for part in range(2):
            cols = pl.ds(part * half, half)
            q = qh[c, pl.ds(part * half, half), :]
            total = acc[c, :, cols]
            for tier in range(TIERS):
                row = lw[LOCAL_BITS + 1 + tier, pl.ds(c, 1), cols] * (
                    switches[tier] * FACTOR[LOCAL_BITS + 1 + tier]
                )
                total = total + dot_nt(buckets[tier], q) * row
            heads[c, pl.ds(part * half, half), :] = total.astype(BF16).T

    def active(t, start):
        return jnp.logical_and(t >= start, t < start + H)

    def by_position(half):
        some = pl.ds(half * HALF, HALF)

        def step(i, carry):
            out[strip(i), some, :] = jnp.transpose(heads[some, strip(i), :], (1, 0, 2))
            return carry

        lax.fori_loop(0, T // STRIP, step, 0)

    def tick(t, carry):
        @pl.when(active(t, 0))
        def _():
            values = vh[t].T
            vt[t] = values
            state = dot_nn(values, kh[t])
            run[t] = state
            sent[0, t] = state.astype(BF16)

        for stage in reversed(range(1, STAGES)):
            @pl.when(active(t, DELAY[stage]))
            def _(stage=stage):
                c = t - DELAY[stage]
                receive(stage - 1, c)
                if stage == 4:
                    other = got[4, c].astype(F32) + got[8, c].astype(F32)
                    got[4, c] = other.astype(BF16)
                    total = run[c] + got[3, c].astype(F32) + other
                else:
                    total = run[c] + got[arrivals[stage - 1][0], c].astype(F32)
                run[c] = total
                sent[stage, c] = total.astype(BF16)

        for stage in (4, 5, 3, 2, 1, 0):
            @pl.when(active(t, DELAY[stage]))
            def _(stage=stage):
                start_sends(stage, t - DELAY[stage])

        @pl.when(active(t, LOCAL_AT))
        def _():
            @pl.when(t == LOCAL_AT)
            def _():
                copies[0].wait()
                copies[1].wait()
                lax.fori_loop(0, T // STRIP, unpack_queries, 0)
            local(t - LOCAL_AT)

        @pl.when(active(t, DELAY[STAGES]))
        def _():
            c = t - DELAY[STAGES]
            receive(STAGES - 1, c)
            finish(c)

        @pl.when(t == DELAY[STAGES] + HALF)
        def _():
            by_position(0)

        return carry

    lax.fori_loop(0, TICKS, tick, 0)

    by_position(1)

    for stage in range(STAGES):
        for index, (slot, device, who) in enumerate(routes[stage]):
            whole = pltpu.make_async_remote_copy(
                src_ref=sent.at[stage],
                dst_ref=got.at[slot],
                send_sem=send_sem.at[number[stage, index]],
                recv_sem=recv_sem.at[slot, 0],
                device_id=device,
                device_id_type=MESH,
            )
            guarded(who, whole.wait_send)


def per_device(queries, key_vectors, value_vectors, level_weights):
    hbm = pl.BlockSpec(memory_space=pltpu.HBM)
    return pl.pallas_call(
        kernel,
        out_shape=pltpu.VMEM((T, H, D), BF16),
        in_specs=[hbm] * 4,
        out_specs=pl.BlockSpec(memory_space=pltpu.VMEM),
        scratch_shapes=[
            pltpu.VMEM((T, H, D), BF16),
            pltpu.VMEM((T, H, D), BF16),
            pltpu.VMEM((T, H, D), BF16),
            pltpu.VMEM((LEVELS, H, T), F32),
            pltpu.VMEM((H, T, D), BF16),
            pltpu.VMEM((H, T, D), BF16),
            pltpu.VMEM((H, T, D), BF16),
            pltpu.VMEM((H, D, T), BF16),
            pltpu.VMEM((T, T), BF16),
            pltpu.VMEM((H, D, T), F32),
            pltpu.VMEM((H, T, D), BF16),
            pltpu.VMEM((H, D, D), F32),
            pltpu.VMEM((STAGES, H, D, D), BF16),
            pltpu.VMEM((SLOTS, H, D, D), BF16),
            pltpu.SemaphoreType.DMA((2,)),
            pltpu.SemaphoreType.DMA((T // STRIP,)),
            pltpu.SemaphoreType.DMA((T // STRIP,)),
            pltpu.SemaphoreType.DMA((12,)),
            pltpu.SemaphoreType.DMA((SLOTS, H)),
        ],
        compiler_params=pltpu.CompilerParams(
            collective_id=0, has_side_effects=True, vmem_limit_bytes=64_500_000
        ),
    )(queries, key_vectors, value_vectors, level_weights)


def solution(mesh):
    placed = (
        P(("outer", "inner"), None, None),
        P(("outer", "inner"), None, None),
        P(("outer", "inner"), None, None),
        P(None, None, ("outer", "inner")),
    )
    return jax.shard_map(
        per_device,
        mesh=mesh,
        in_specs=placed,
        out_specs=P(("outer", "inner"), None, None),
        check_vma=False,
    )
```
